256 devices in a mesh: pipe: 4 (over x), seq: 64 (over y, z, core).
Axes of the slice: x: 4, y: 4, z: 8, core: 2. Of those that a mesh axis runs over, the one named last changes fastest.
Arguments:
- arriving: bfloat16 [4, 65536, 2048], P('pipe', 'seq'), may hold values from -6 to 6
- loss_grad: bfloat16 [65536, 2048], P('seq', 'pipe'), may hold values from -6 to 6
- first_blocks: bfloat16 [4, 256, 256, 256], P('pipe', 'seq'), may hold values from -0.375 to 0.375
- second_blocks: bfloat16 [4, 256, 256, 256], P('pipe', 'seq'), may hold values from -0.375 to 0.375
- inner_gain: bfloat16 [4, 2048], P('pipe'), may hold values from 0.25 to 1.75
- outer_gain: bfloat16 [4, 2048], P('pipe'), may hold values from 0.25 to 1.75
Outputs:
- entering: bfloat16 [4, 65536, 2048], P('pipe', 'seq')
- leaving: bfloat16 [65536, 2048], P('seq', 'pipe')
The draws below stay inside these ranges and needn't reach their ends.
All inputs are finite; a program needn't handle non-finite values.
Results may differ from the reference program's by a relative error of at most 0.0059.
Values may be sent and summed in bfloat16 or wider, within the bound.
No kernel may reach another device: no remote copies, remote signals or barrier semaphores. Data moves between devices by JAX's collectives and lax.ppermute only.
A program may use at most 128 MiB of HBM per device.

```python
import jax
import jax.numpy as jnp

D = 2048
NB = 256
L = 65536
N_PIPE = 4


def steps_of(stream_key, shape, pieces, least, largest):
    loudness, own = 1.0, jax.random.fold_in(stream_key, 6)
    for axis_at, parts in pieces:
        steps = jnp.exp(jax.random.uniform(jax.random.fold_in(own, axis_at), (parts,), jnp.float32, least / len(pieces), largest / len(pieces)))
        loudness = loudness * jnp.repeat(steps, shape[axis_at] // parts).reshape([-1 if axis == axis_at else 1 for axis in range(len(shape))])
    return loudness


def normal_values(own_key, shape, scale, bound, split=(), dtype=jnp.bfloat16):
    array = scale * jax.random.normal(own_key, shape, jnp.float32)
    if split:
        array = array * steps_of(own_key, shape, split, -0.22, 0.18)
    return jnp.clip(array, -bound, bound).astype(dtype)


def setup_inputs(seed: int = 0) -> dict:
    splits = jax.random.split(jax.random.key(seed), 7)
    arriving = normal_values(splits[0], (N_PIPE, L, D), 1.0, 6.0, ((0, 4), (1, 64)))
    loss_grad = normal_values(splits[1], (L, D), 1.0, 6.0, ((0, 64), (1, 4)))
    first_blocks = normal_values(splits[2], (N_PIPE, NB, NB, NB), NB ** -0.5, 0.375, ((0, 4), (1, 64)))
    second_blocks = normal_values(splits[3], (N_PIPE, NB, NB, NB), NB ** -0.5, 0.375, ((0, 4), (1, 64)))
    inner_gain = jnp.clip(1.0 + 0.15 * jax.random.normal(splits[4], (N_PIPE, D), jnp.float32), 0.25, 1.75).astype(jnp.bfloat16)
    outer_gain = jnp.clip(1.0 + 0.15 * jax.random.normal(splits[5], (N_PIPE, D), jnp.float32), 0.25, 1.75).astype(jnp.bfloat16)
    return {"arriving": arriving, "loss_grad": loss_grad, "first_blocks": first_blocks, "second_blocks": second_blocks, "inner_gain": inner_gain, "outer_gain": outer_gain}


def mixer(gradient, first_part, second_part, inner_part, outer_part):
    blocked = gradient.reshape(NB, NB, D).astype(jnp.float32)
    scaled = (blocked * inner_part.astype(jnp.float32)).astype(jnp.bfloat16)
    mixed = jnp.einsum("kjc,jki->ijc", scaled.astype(jnp.float32), second_part.astype(jnp.float32)).astype(jnp.bfloat16)
    spread = jnp.einsum("ikc,ikj->ijc", mixed.astype(jnp.float32), first_part.astype(jnp.float32))
    result = blocked + outer_part.astype(jnp.float32) * spread
    return result.astype(jnp.bfloat16).reshape(NB * NB, D)


def reference(arriving, loss_grad, first_blocks, second_blocks, inner_gain, outer_gain):
    passed = []
    for section in range(N_PIPE):
        passed.append(mixer(arriving[section], first_blocks[section], second_blocks[section], inner_gain[section], outer_gain[section]))
    entering = []
    for section in range(N_PIPE):
        if section < N_PIPE - 1:
            source = passed[section + 1]
        else:
            source = loss_grad
        entering.append(mixer(source, first_blocks[section], second_blocks[section], inner_gain[section], outer_gain[section]))
    return jnp.stack(entering, axis=0), passed[0]
```

```python
import jax
import jax.numpy as jnp
from jax import lax
from jax.sharding import PartitionSpec as P

CHUNKS = 2


def to_columns(gradient, inner):
    scaled = (gradient.astype(jnp.float32) * inner.astype(jnp.float32)).astype(jnp.bfloat16)
    return lax.all_to_all(scaled, "seq", split_axis=1, concat_axis=0, tiled=True)


def to_rows(columns, second):
    mixed = jnp.einsum("kjc,jki->ijc", columns, second, preferred_element_type=jnp.float32)
    return lax.all_to_all(mixed.astype(jnp.bfloat16), "seq", split_axis=0, concat_axis=1, tiled=True)


def finish(gradient, rows, first, outer):
    spread = jnp.einsum("ikc,ikj->ijc", rows, first, preferred_element_type=jnp.float32)
    result = gradient.astype(jnp.float32) + outer.astype(jnp.float32) * spread
    return result.astype(jnp.bfloat16)


def per_device(arriving, loss_grad, first_blocks, second_blocks, inner_gain, outer_gain):
    sections = lax.axis_size("pipe")
    position = lax.axis_index("pipe")
    last = sections - 1
    first, second = first_blocks[0], second_blocks[0]
    count, order = first.shape[0], first.shape[1]
    channels = arriving.shape[2]
    piece = loss_grad.shape[1]
    width = channels // CHUNKS
    whole = arriving[0].reshape(count, order, channels)
    loss = loss_grad.reshape(count, order, piece)

    parts = [slice(n * width, (n + 1) * width) for n in range(CHUNKS)]
    inner = [inner_gain[:, p] for p in parts]
    outer = [outer_gain[:, p] for p in parts]
    source = [whole[:, :, p] for p in parts]

    lost = []
    for q in range(sections):
        lost.append(loss if q == last else lax.ppermute(loss, "pipe", [(q, last)]))

    def layer(grads):
        columns = [to_columns(g, a) for g, a in zip(grads, inner)]
        rows = [to_rows(c, second) for c in columns]
        return [finish(g, r, first, b) for g, r, b in zip(grads, rows, outer)]

    passed = layer(source)
    back = [(i + 1, i) for i in range(sections - 1)]
    nexts, leaves = [], []
    per_chunk = width // piece
    for n in range(CHUNKS):
        moved = lax.ppermute(passed[n], "pipe", back)
        loss_part = jnp.concatenate(lost[n * per_chunk:(n + 1) * per_chunk], axis=2)
        nexts.append(jnp.where(position == last, loss_part, moved))
        for m in range(per_chunk):
            q = n * per_chunk + m
            mine = passed[n][:, :, m * piece:(m + 1) * piece]
            leaves.append(mine if q == 0 else lax.ppermute(mine, "pipe", [(0, q)]))
    leaving = leaves[0]
    for q in range(1, sections):
        leaving = jnp.where(position == q, leaves[q], leaving)
    entering = jnp.concatenate(layer(nexts), axis=2)
    return entering.reshape(arriving.shape), leaving.reshape(loss_grad.shape)


def solution(mesh):
    placed = (
        P("pipe", "seq", None),
        P("seq", "pipe"),
        P("pipe", "seq", None, None),
        P("pipe", "seq", None, None),
        P("pipe", None),
        P("pipe", None),
    )
    return jax.shard_map(
        per_device,
        mesh=mesh,
        in_specs=placed,
        out_specs=(P("pipe", "seq", None), P("seq", "pipe")),
        check_vma=False,
    )
```

```python
import jax
import jax.numpy as jnp
from jax import lax
from jax.sharding import PartitionSpec as P

F32, BF16 = jnp.float32, jnp.bfloat16


def dot(a, b):
    return lax.dot_general(a, b, (((1,), (0,)), ((), ())), preferred_element_type=F32)


def exchange(rows, devices):
    tile = rows.shape[0] // devices
    blocks = rows.reshape(devices, tile, rows.shape[1])
    return lax.all_to_all(blocks, "seq", split_axis=0, concat_axis=0).reshape(rows.shape)


def per_device(arriving, loss_grad, first_blocks, second_blocks, inner_gain, outer_gain):
    sections = lax.axis_size("pipe")
    devices = lax.axis_size("seq")
    position = lax.axis_index("pipe")
    last = sections - 1
    first, second = first_blocks[0], second_blocks[0]
    count, order = first.shape[0], first.shape[1]
    rows, channels = arriving.shape[1:]
    piece = loss_grad.shape[1]
    tile = count * count

    out = lax.broadcasted_iota(jnp.int32, (rows, rows), 0)
    into = lax.broadcasted_iota(jnp.int32, (rows, rows), 1)
    natural = (out // count % count) * order + (out // tile) * count + out % count
    permutation = (into == natural).astype(BF16)

    at = lax.broadcasted_iota(jnp.int32, (count, rows, order), 1)
    col = lax.broadcasted_iota(jnp.int32, (count, rows, order), 2)
    own = lax.broadcasted_iota(jnp.int32, (count, rows, order), 0)
    place = (at == col * count + own).astype(BF16)
    tall = jnp.einsum("jni,jki->nk", place, second, preferred_element_type=F32).astype(BF16)
    k = lax.broadcasted_iota(jnp.int32, (order, rows), 0)
    r = lax.broadcasted_iota(jnp.int32, (order, rows), 1)
    wide = dot(tall, (k == r // count).astype(BF16))
    second_spread = jnp.where(out % count == into % count, wide, 0.0).astype(BF16)

    pick = (k == (r // tile) * count + r % count).astype(BF16)
    wide = jnp.einsum("ikj,kr->ijr", first, pick, preferred_element_type=F32).reshape(rows, rows)
    first_spread = jnp.where(out // order == into // count % count, wide, 0.0).astype(BF16)

    inner, outer = inner_gain.astype(F32), outer_gain.astype(F32)

    def send(gradient, cols):
        scaled = (gradient.astype(F32) * inner[:, cols]).astype(BF16)
        return exchange(dot(permutation, scaled).astype(BF16), devices)

    def mix(columns):
        return dot(second_spread, columns).astype(BF16)

    def finish(gradient, returned, cols):
        spread = dot(first_spread, returned)
        return (gradient.astype(F32) + outer[:, cols] * spread).astype(BF16)

    whole = slice(0, channels)
    halves = (slice(0, channels // 2), slice(channels // 2, channels))
    gradient = arriving[0]

    lost = [loss_grad if q == last else lax.ppermute(loss_grad, "pipe", [(q, last)]) for q in range(sections)]
    columns, lost = lax.optimization_barrier((send(gradient, whole), lost))

    returned = [exchange(mix(columns[:, h]), devices) for h in halves]
    back = [(i + 1, i) for i in range(sections - 1)]
    sources, leaves, sent = [], [], []
    per_half = sections // 2
    for n, h in enumerate(halves):
        passed = finish(gradient[:, h], returned[n], h)
        moved = lax.ppermute(passed, "pipe", back)
        here = jnp.concatenate(lost[n * per_half:(n + 1) * per_half], axis=1)
        sources.append(jnp.where(position == last, here, moved))
        for m in range(per_half):
            q = n * per_half + m
            mine = passed[:, m * piece:(m + 1) * piece]
            leaves.append(mine if q == 0 else lax.ppermute(mine, "pipe", [(0, q)]))
        sent.append(send(sources[n], h))

    leaving = leaves[0]
    for q in range(1, sections):
        leaving = jnp.where(position == q, leaves[q], leaving)
    mixed, leaving = lax.optimization_barrier((mix(jnp.concatenate(sent, axis=1)), leaving))
    final = exchange(mixed, devices)
    entering = finish(jnp.concatenate(sources, axis=1), final, whole)
    return entering[None], leaving


def solution(mesh):
    placed = (
        P("pipe", "seq", None),
        P("seq", "pipe"),
        P("pipe", "seq", None, None),
        P("pipe", "seq", None, None),
        P("pipe", None),
        P("pipe", None),
    )
    return jax.shard_map(
        per_device,
        mesh=mesh,
        in_specs=placed,
        out_specs=(P("pipe", "seq", None), P("seq", "pipe")),
        check_vma=False,
    )
```

```python
import jax
import jax.numpy as jnp
from jax import lax
from jax.experimental import pallas as pl
from jax.sharding import PartitionSpec as P

F32, BF16 = jnp.float32, jnp.bfloat16


def dot(a, b):
    return lax.dot_general(a, b, (((1,), (0,)), ((), ())), preferred_element_type=F32)


def exchange(rows, devices):
    tile = rows.shape[0] // devices
    blocks = rows.reshape(devices, tile, rows.shape[1])
    return lax.all_to_all(blocks, "seq", split_axis=0, concat_axis=0).reshape(rows.shape)


def product_kernel(weights, columns, *rest):
    rest[-1][...] = dot(weights[...], columns[...]).astype(BF16)


def product_into(weights, columns, total, at, buffer=None):
    rows, depth = weights.shape
    width = min(512, columns.shape[1])
    steps, first = columns.shape[1] // width, at // width
    in_specs = [
        pl.BlockSpec((rows, depth), lambda n: (0, 0), pipeline_mode=pl.Buffered(1)),
        pl.BlockSpec((depth, width), lambda n: (0, n)),
    ]
    operands = [weights, columns]
    aliases = {}
    if buffer is not None:
        in_specs.append(pl.BlockSpec(memory_space=pl.ANY))
        operands.append(buffer)
        aliases = {2: 0}
    return pl.pallas_call(
        product_kernel,
        out_shape=jax.ShapeDtypeStruct((rows, total), BF16),
        grid=(steps,),
        in_specs=in_specs,
        out_specs=pl.BlockSpec((rows, width), lambda n: (0, first + n)),
        input_output_aliases=aliases,
        cost_estimate=pl.CostEstimate(
            flops=2 * rows * depth * columns.shape[1],
            bytes_accessed=2 * (rows * depth + 2 * rows * columns.shape[1]),
            transcendentals=0,
        ),
    )(*operands)


def per_device(arriving, loss_grad, first_blocks, second_blocks, inner_gain, outer_gain):
    sections = lax.axis_size("pipe")
    devices = lax.axis_size("seq")
    position = lax.axis_index("pipe")
    last = sections - 1
    first, second = first_blocks[0], second_blocks[0]
    count, order = first.shape[0], first.shape[1]
    rows, channels = arriving.shape[1:]
    piece = loss_grad.shape[1]
    tile = count * count

    out = lax.broadcasted_iota(jnp.int32, (rows, rows), 0)
    into = lax.broadcasted_iota(jnp.int32, (rows, rows), 1)
    natural = (out // count % count) * order + (out // tile) * count + out % count
    permutation = (into == natural).astype(BF16)

    at = lax.broadcasted_iota(jnp.int32, (count, rows, order), 1)
    col = lax.broadcasted_iota(jnp.int32, (count, rows, order), 2)
    own = lax.broadcasted_iota(jnp.int32, (count, rows, order), 0)
    place = (at == col * count + own).astype(BF16)
    tall = jnp.einsum("jni,jki->nk", place, second, preferred_element_type=F32).astype(BF16)
    k = lax.broadcasted_iota(jnp.int32, (order, rows), 0)
    r = lax.broadcasted_iota(jnp.int32, (order, rows), 1)
    wide = dot(tall, (k == r // count).astype(BF16))
    second_spread = jnp.where(out % count == into % count, wide, 0.0).astype(BF16)

    pick = (k == (r // tile) * count + r % count).astype(BF16)
    wide = jnp.einsum("ikj,kr->ijr", first, pick, preferred_element_type=F32).reshape(rows, rows)
    first_spread = jnp.where(out // order == into // count % count, wide, 0.0).astype(BF16)

    inner, outer = inner_gain.astype(F32), outer_gain.astype(F32)
    restore = (natural.T == into.T).astype(BF16)
    first_sent = dot(permutation, first_spread).astype(BF16)

    def scale(gradient, cols):
        return (gradient.astype(F32) * inner[:, cols]).astype(BF16)

    def mix(columns):
        return dot(second_spread, columns).astype(BF16)

    def finish(gradient, weights, returned, cols):
        spread = dot(weights, returned)
        return (gradient.astype(F32) + outer[:, cols] * spread).astype(BF16)

    whole = slice(0, channels)
    halves = (slice(0, channels // 2), slice(channels // 2, channels))
    pieces = [slice(q * piece, (q + 1) * piece) for q in range(sections)]
    per_half = sections // 2

    reordered = dot(permutation, arriving[0]).astype(BF16)
    first_sending = exchange(scale(reordered, whole), devices)

    loss_sent = dot(permutation, loss_grad).astype(BF16)
    lost = [loss_sent if q == last else lax.ppermute(loss_sent, "pipe", [(q, last)]) for q in range(sections)]
    columns, lost, first_sent = lax.optimization_barrier((first_sending, lost, first_sent))

    back = [(i + 1, i) for i in range(sections - 1)]
    returned = [exchange(mix(columns[:, h]), devices) for h in halves]
    passed, sources, sent = [], [], []
    for n, h in enumerate(halves):
        moved = []
        for m in range(per_half):
            q = n * per_half + m
            passed.append(finish(reordered[:, pieces[q]], first_sent, returned[n][:, m * piece:(m + 1) * piece], pieces[q]))
            moved.append(lax.ppermute(passed[q], "pipe", back))
        here = lost[n * per_half:(n + 1) * per_half]
        both = [jnp.where(position == last, a, b) for a, b in zip(here, moved)]
        sources.append(jnp.concatenate(both, axis=1))
        sent.append(exchange(scale(sources[n], h), devices))

    leaving = passed[0]
    for q in range(1, sections):
        leaving = jnp.where(position == q, lax.ppermute(passed[q], "pipe", [(0, q)]), leaving)
    leaving = dot(restore, leaving).astype(BF16)

    mixed = product_into(second_spread, sent[0], channels, 0)
    mixed = product_into(second_spread, sent[1], channels, channels // 2, mixed)
    mixed, leaving = lax.optimization_barrier((mixed, leaving))
    final = exchange(mixed, devices)
    source = dot(restore, jnp.concatenate(sources, axis=1)).astype(BF16)
    final, source = lax.optimization_barrier((final, source))
    entering = finish(source, first_spread, final, whole)
    return entering[None], leaving


def solution(mesh):
    placed = (
        P("pipe", "seq", None),
        P("seq", "pipe"),
        P("pipe", "seq", None, None),
        P("pipe", "seq", None, None),
        P("pipe", None),
        P("pipe", None),
    )
    return jax.shard_map(
        per_device,
        mesh=mesh,
        in_specs=placed,
        out_specs=(P("pipe", "seq", None), P("seq", "pipe")),
        check_vma=False,
    )
```

```python
import functools

import jax
import jax.numpy as jnp
from jax import lax
from jax.experimental import pallas as pl
from jax.experimental.pallas import tpu as pltpu
from jax.sharding import PartitionSpec as P


F32, BF16 = jnp.float32, jnp.bfloat16


def dot(a, b):
    return lax.dot_general(a, b, (((1,), (0,)), ((), ())), preferred_element_type=F32)


def exchange(rows, devices):
    tile = rows.shape[0] // devices
    blocks = rows.reshape(devices, tile, rows.shape[1])
    blocks = lax.all_to_all(blocks, "seq", split_axis=0, concat_axis=0)
    return blocks.reshape(rows.shape)


def reorder_kernel(count, gain, rows_in, rows_out):
    order = rows_in.shape[0] // count
    chunk, tile = order // count, count * count
    n = lax.broadcasted_iota(jnp.int32, (order, order), 0)
    m = lax.broadcasted_iota(jnp.int32, (order, order), 1)
    place = (m == (n // count % count) * chunk + (n // tile) * count + n % count).astype(BF16)
    for group in range(count):
        starts = [il * order + group * chunk for il in range(count)]
        taken = jnp.concatenate([rows_in[s:s + chunk, :] for s in starts], axis=0)
        if gain is not None:
            taken = (taken.astype(F32) * gain[...]).astype(BF16)
        rows_out[group * order:(group + 1) * order, :] = dot(place, taken).astype(BF16)


def reorder(rows_in, count, gain=None):
    rows, channels = rows_in.shape
    width = min(1024, channels)
    specs = [pl.BlockSpec((rows, width), lambda n: (0, n))]
    operands = [rows_in]
    kernel = functools.partial(reorder_kernel, count, None)
    if gain is not None:
        specs.insert(0, pl.BlockSpec((1, width), lambda n: (0, n)))
        operands.insert(0, gain)
        kernel = functools.partial(reorder_kernel, count)
    return pl.pallas_call(
        kernel,
        out_shape=jax.ShapeDtypeStruct(rows_in.shape, BF16),
        grid=(channels // width,),
        in_specs=specs,
        out_specs=pl.BlockSpec((rows, width), lambda n: (0, n)),
        cost_estimate=pl.CostEstimate(
            flops=2 * rows * (rows // count) * channels, bytes_accessed=4 * rows * channels, transcendentals=0
        ),
    )(*operands)


def scale_kernel(flag, gain, here, moved, *rest):
    gradient = jnp.where(flag[0] == 1, here[...].astype(F32), moved[...].astype(F32))
    rest[-1][...] = (gradient * gain[...]).astype(BF16)


def scale_into(flag, gain, here, moved, total, at, buffer=None):
    rows, width = here.shape
    step, column = rows // 4, at // width
    block = pl.BlockSpec((step, width), lambda n: (n, 0))
    in_specs = [
        pl.BlockSpec(memory_space=pltpu.SMEM),
        pl.BlockSpec((1, width), lambda n: (0, 0)),
        block,
        block,
    ]
    operands = [flag, gain, here, moved]
    aliases = {}
    if buffer is not None:
        in_specs.append(pl.BlockSpec(memory_space=pl.ANY))
        operands.append(buffer)
        aliases = {4: 0}
    return pl.pallas_call(
        scale_kernel,
        out_shape=jax.ShapeDtypeStruct((rows, total), BF16),
        grid=(4,),
        in_specs=in_specs,
        out_specs=pl.BlockSpec((step, width), lambda n: (n, column)),
        input_output_aliases=aliases,
        cost_estimate=pl.CostEstimate(flops=rows * width, bytes_accessed=6 * rows * width, transcendentals=0),
    )(*operands)


def product_kernel(weights, columns, *rest):
    rest[-1][...] = dot(weights[...], columns[...]).astype(BF16)


def product_into(weights, columns, total, at, buffer=None):
    rows, depth = weights.shape
    width = min(512, columns.shape[1])
    steps, first = columns.shape[1] // width, at // width
    in_specs = [
        pl.BlockSpec((rows, depth), lambda n: (0, 0), pipeline_mode=pl.Buffered(1)),
        pl.BlockSpec((depth, width), lambda n: (0, n)),
    ]
    operands = [weights, columns]
    aliases = {}
    if buffer is not None:
        in_specs.append(pl.BlockSpec(memory_space=pl.ANY))
        operands.append(buffer)
        aliases = {2: 0}
    return pl.pallas_call(
        product_kernel,
        out_shape=jax.ShapeDtypeStruct((rows, total), BF16),
        grid=(steps,),
        in_specs=in_specs,
        out_specs=pl.BlockSpec((rows, width), lambda n: (0, first + n)),
        input_output_aliases=aliases,
        cost_estimate=pl.CostEstimate(
            flops=2 * rows * depth * columns.shape[1],
            bytes_accessed=2 * (rows * depth + 2 * rows * columns.shape[1]),
            transcendentals=0,
        ),
    )(*operands)


def local_program(arriving, loss_grad, first_blocks, second_blocks, inner_gain, outer_gain):
    sections = lax.axis_size("pipe")
    devices = lax.axis_size("seq")
    position = lax.axis_index("pipe")
    last = sections - 1
    first, second = first_blocks[0], second_blocks[0]
    count, order = first.shape[0], first.shape[1]
    rows, channels = arriving.shape[1:]
    piece = loss_grad.shape[1]
    tile = count * count

    out = lax.broadcasted_iota(jnp.int32, (rows, rows), 0)
    into = lax.broadcasted_iota(jnp.int32, (rows, rows), 1)
    natural = (out // count % count) * order + (out // tile) * count + out % count

    at = lax.broadcasted_iota(jnp.int32, (count, rows, order), 1)
    col = lax.broadcasted_iota(jnp.int32, (count, rows, order), 2)
    own = lax.broadcasted_iota(jnp.int32, (count, rows, order), 0)
    place = (at == col * count + own).astype(BF16)
    tall = jnp.einsum("jni,jki->nk", place, second, preferred_element_type=F32).astype(BF16)
    k = lax.broadcasted_iota(jnp.int32, (order, rows), 0)
    r = lax.broadcasted_iota(jnp.int32, (order, rows), 1)
    wide = dot(tall, (k == r // count).astype(BF16))
    second_spread = jnp.where(out % count == into % count, wide, 0.0).astype(BF16)

    pick = (k == (r // tile) * count + r % count).astype(BF16)
    wide = jnp.einsum("ikj,kr->ijr", first, pick, preferred_element_type=F32).reshape(rows, rows)
    first_spread = jnp.where(out // order == into // count % count, wide, 0.0).astype(BF16)

    inner, outer = inner_gain.astype(F32), outer_gain.astype(F32)
    restore = (natural.T == into.T).astype(BF16)
    first_sent = reorder(first_spread, count)

    def mix(columns):
        return dot(second_spread, columns).astype(BF16)

    def finish(gradient, weights, returned, cols):
        spread = dot(weights, returned)
        return (gradient.astype(F32) + outer[:, cols] * spread).astype(BF16)

    whole = slice(0, channels)
    halves = (slice(0, channels // 2), slice(channels // 2, channels))
    pieces = [slice(q * piece, (q + 1) * piece) for q in range(sections)]
    per_half = sections // 2

    first_sending = exchange(reorder(arriving[0], count, inner), devices)

    reordered = reorder(arriving[0], count)
    loss_sent = reorder(loss_grad, count)
    lost = [loss_sent if q == last else lax.ppermute(loss_sent, "pipe", [(q, last)]) for q in range(sections)]
    columns, lost, first_sent, reordered = lax.optimization_barrier((first_sending, lost, first_sent, reordered))

    back = [(i + 1, i) for i in range(sections - 1)]
    returned = [exchange(mix(columns[:, h]), devices) for h in halves]
    flag = (position == last).astype(jnp.int32).reshape(1)

    def step(q):
        cut = slice(q % per_half * piece, (q % per_half + 1) * piece)
        result = finish(reordered[:, pieces[q]], first_sent, returned[q // per_half][:, cut], pieces[q])
        return result, lax.ppermute(result, "pipe", back)

    def fill(buffer, q):
        at = q % per_half * piece
        return scale_into(flag, inner[:, pieces[q]], lost[q], moved[q], channels // 2, at, buffer)

    passed, moved, sent = [None] * sections, [None] * sections, []
    for q in range(per_half):
        passed[q], moved[q] = step(q)
    buffer = None
    for q in range(per_half):
        buffer = fill(buffer, q)
    passed[per_half], moved[per_half] = step(per_half)
    buffer, passed[per_half] = lax.optimization_barrier((buffer, passed[per_half]))
    sent.append(exchange(buffer, devices))
    for q in range(per_half + 1, sections):
        passed[q], moved[q] = step(q)
    buffer = None
    for q in range(per_half, sections):
        buffer = fill(buffer, q)
    sent.append(exchange(buffer, devices))

    leaving = passed[0]
    for q in range(1, sections):
        leaving = jnp.where(position == q, lax.ppermute(passed[q], "pipe", [(0, q)]), leaving)
    leaving = dot(restore, leaving).astype(BF16)

    mixed = product_into(second_spread, sent[0], channels, 0)
    mixed = product_into(second_spread, sent[1], channels, channels // 2, mixed)
    final = exchange(mixed, devices)
    source = jnp.concatenate([jnp.where(position == last, a, b) for a, b in zip(lost, moved)], axis=1)
    source = dot(restore, source).astype(BF16)
    final, source, leaving = lax.optimization_barrier((final, source, leaving))
    entering = finish(source, first_spread, final, whole)
    return entering[None], leaving


def solution(mesh):
    placed = (
        P("pipe", "seq", None),
        P("seq", "pipe"),
        P("pipe", "seq", None, None),
        P("pipe", "seq", None, None),
        P("pipe", None),
        P("pipe", None),
    )
    return jax.shard_map(
        local_program,
        mesh=mesh,
        in_specs=placed,
        out_specs=(P("pipe", "seq", None), P("seq", "pipe")),
        check_vma=False,
    )
```

```python
import functools

import jax
import jax.numpy as jnp
from jax import lax
from jax.experimental import pallas as pl
from jax.experimental.pallas import tpu as pltpu
from jax.sharding import PartitionSpec as P


F32, BF16 = jnp.float32, jnp.bfloat16


def dot(a, b):
    return lax.dot_general(a, b, (((1,), (0,)), ((), ())), preferred_element_type=F32)


def exchange(rows, devices):
    tile = rows.shape[0] // devices
    blocks = rows.reshape(devices, tile, rows.shape[1])
    blocks = lax.all_to_all(blocks, "seq", split_axis=0, concat_axis=0)
    return blocks.reshape(rows.shape)


def reorder_kernel(count, gain, rows_in, rows_out):
    order = rows_in.shape[0] // count
    chunk, tile = order // count, count * count
    n = lax.broadcasted_iota(jnp.int32, (order, order), 0)
    m = lax.broadcasted_iota(jnp.int32, (order, order), 1)
    place = (m == (n // count % count) * chunk + (n // tile) * count + n % count).astype(BF16)
    for group in range(count):
        starts = [il * order + group * chunk for il in range(count)]
        taken = jnp.concatenate([rows_in[s:s + chunk, :] for s in starts], axis=0)
        if gain is not None:
            taken = (taken.astype(F32) * gain[...].astype(F32)).astype(BF16)
        rows_out[group * order:(group + 1) * order, :] = dot(place, taken).astype(BF16)


def reorder(rows_in, count, gain=None):
    rows, channels = rows_in.shape
    width = min(1024, channels)
    specs = [pl.BlockSpec((rows, width), lambda n: (0, n))]
    operands = [rows_in]
    kernel = functools.partial(reorder_kernel, count, None)
    if gain is not None:
        specs.insert(0, pl.BlockSpec((1, width), lambda n: (0, n)))
        operands.insert(0, gain)
        kernel = functools.partial(reorder_kernel, count)
    return pl.pallas_call(
        kernel,
        out_shape=jax.ShapeDtypeStruct(rows_in.shape, BF16),
        grid=(channels // width,),
        in_specs=specs,
        out_specs=pl.BlockSpec((rows, width), lambda n: (0, n)),
        cost_estimate=pl.CostEstimate(
            flops=2 * rows * (rows // count) * channels, bytes_accessed=4 * rows * channels, transcendentals=0
        ),
    )(*operands)


def scale_kernel(flag, gain, here, moved, *rest):
    gradient = jnp.where(flag[0] == 1, here[...].astype(F32), moved[...].astype(F32))
    rest[-1][...] = (gradient * gain[...].astype(F32)).astype(BF16)


def scale_into(flag, gain, here, moved, total, at, buffer=None):
    rows, width = here.shape
    step, column = rows // 2, at // width
    block = pl.BlockSpec((step, width), lambda n: (n, 0))
    in_specs = [
        pl.BlockSpec(memory_space=pltpu.SMEM),
        pl.BlockSpec((1, width), lambda n: (0, 0)),
        block,
        block,
    ]
    operands = [flag, gain, here, moved]
    aliases = {}
    if buffer is not None:
        in_specs.append(pl.BlockSpec(memory_space=pl.ANY))
        operands.append(buffer)
        aliases = {4: 0}
    return pl.pallas_call(
        scale_kernel,
        out_shape=jax.ShapeDtypeStruct((rows, total), BF16),
        grid=(2,),
        in_specs=in_specs,
        out_specs=pl.BlockSpec((step, width), lambda n: (n, column)),
        input_output_aliases=aliases,
        cost_estimate=pl.CostEstimate(flops=rows * width, bytes_accessed=6 * rows * width, transcendentals=0),
    )(*operands)


def product_kernel(weights, columns, *rest):
    rest[-1][...] = dot(weights[...], columns[...]).astype(BF16)


def product_into(weights, columns, total, at, buffer=None):
    rows, depth = weights.shape
    width = min(512, columns.shape[1])
    steps, first = columns.shape[1] // width, at // width
    in_specs = [
        pl.BlockSpec((rows, depth), lambda n: (0, 0), pipeline_mode=pl.Buffered(1)),
        pl.BlockSpec((depth, width), lambda n: (0, n)),
    ]
    operands = [weights, columns]
    aliases = {}
    if buffer is not None:
        in_specs.append(pl.BlockSpec(memory_space=pl.ANY))
        operands.append(buffer)
        aliases = {2: 0}
    return pl.pallas_call(
        product_kernel,
        out_shape=jax.ShapeDtypeStruct((rows, total), BF16),
        grid=(steps,),
        in_specs=in_specs,
        out_specs=pl.BlockSpec((rows, width), lambda n: (0, first + n)),
        input_output_aliases=aliases,
        cost_estimate=pl.CostEstimate(
            flops=2 * rows * depth * columns.shape[1],
            bytes_accessed=2 * (rows * depth + 2 * rows * columns.shape[1]),
            transcendentals=0,
        ),
    )(*operands)


def local_program(arriving, loss_grad, first_blocks, second_blocks, inner_gain, outer_gain):
    sections = lax.axis_size("pipe")
    devices = lax.axis_size("seq")
    position = lax.axis_index("pipe")
    last = sections - 1
    first, second = first_blocks[0], second_blocks[0]
    count, order = first.shape[0], first.shape[1]
    rows, channels = arriving.shape[1:]
    piece = loss_grad.shape[1]
    tile = count * count

    out = lax.broadcasted_iota(jnp.int32, (rows, rows), 0)
    into = lax.broadcasted_iota(jnp.int32, (rows, rows), 1)
    natural = (out // count % count) * order + (out // tile) * count + out % count

    at = lax.broadcasted_iota(jnp.int32, (count, rows, order), 1)
    col = lax.broadcasted_iota(jnp.int32, (count, rows, order), 2)
    own = lax.broadcasted_iota(jnp.int32, (count, rows, order), 0)
    place = (at == col * count + own).astype(BF16)
    tall = jnp.einsum("jni,jki->nk", place, second, preferred_element_type=F32).astype(BF16)
    k = lax.broadcasted_iota(jnp.int32, (order, rows), 0)
    r = lax.broadcasted_iota(jnp.int32, (order, rows), 1)
    wide = dot(tall, (k == r // count).astype(BF16))
    second_spread = jnp.where(out % count == into % count, wide, 0.0).astype(BF16)

    pick = (k == (r // tile) * count + r % count).astype(BF16)
    wide = jnp.einsum("ikj,kr->ijr", first, pick, preferred_element_type=F32).reshape(rows, rows)
    first_spread = jnp.where(out // order == into // count % count, wide, 0.0).astype(BF16)

    inner, outer = inner_gain, outer_gain.astype(F32)
    restore = (natural.T == into.T).astype(BF16)
    first_sent = reorder(first_spread, count)

    def mix(columns):
        return dot(second_spread, columns).astype(BF16)

    def finish(gradient, weights, returned, cols):
        spread = dot(weights, returned)
        return (gradient.astype(F32) + outer[:, cols] * spread).astype(BF16)

    whole = slice(0, channels)
    halves = (slice(0, channels // 2), slice(channels // 2, channels))
    pieces = [slice(q * piece, (q + 1) * piece) for q in range(sections)]
    per_half = sections // 2

    first_sending = exchange(reorder(arriving[0], count, inner), devices)

    reordered = reorder(arriving[0], count)
    loss_sent = reorder(loss_grad, count)
    lost = [loss_sent if q == last else lax.ppermute(loss_sent, "pipe", [(q, last)]) for q in range(sections)]
    columns, lost, first_sent, reordered = lax.optimization_barrier((first_sending, lost, first_sent, reordered))

    back = [(i + 1, i) for i in range(sections - 1)]
    returned = [exchange(mix(columns[:, h]), devices) for h in halves]
    flag = (position == last).astype(jnp.int32).reshape(1)

    def step(q):
        cut = slice(q % per_half * piece, (q % per_half + 1) * piece)
        result = finish(reordered[:, pieces[q]], first_sent, returned[q // per_half][:, cut], pieces[q])
        return result, lax.ppermute(result, "pipe", back)

    def fill(buffer, q):
        at = q % per_half * piece
        return scale_into(flag, inner[:, pieces[q]], lost[q], moved[q], channels // 2, at, buffer)

    passed, moved, sent = [None] * sections, [None] * sections, []
    for q in range(per_half):
        passed[q], moved[q] = step(q)
    buffer = None
    for q in range(per_half):
        buffer = fill(buffer, q)
    passed[per_half], moved[per_half] = step(per_half)
    sent.append(exchange(buffer, devices))
    for q in range(per_half + 1, sections):
        passed[q], moved[q] = step(q)
    buffer = None
    for q in range(per_half, sections):
        buffer = fill(buffer, q)
    sent.append(exchange(buffer, devices))

    leaving = passed[0]
    for q in range(1, sections):
        leaving = jnp.where(position == q, lax.ppermute(passed[q], "pipe", [(0, q)]), leaving)
    leaving = dot(restore, leaving).astype(BF16)

    mixed = product_into(second_spread, sent[0], channels, 0)
    mixed = product_into(second_spread, sent[1], channels, channels // 2, mixed)
    final = exchange(mixed, devices)
    source = jnp.concatenate([jnp.where(position == last, a, b) for a, b in zip(lost, moved)], axis=1)
    source = dot(restore, source).astype(BF16)
    final, source, leaving = lax.optimization_barrier((final, source, leaving))
    entering = finish(source, first_spread, final, whole)
    return entering[None], leaving


def solution(mesh):
    placed = (
        P("pipe", "seq", None),
        P("seq", "pipe"),
        P("pipe", "seq", None, None),
        P("pipe", "seq", None, None),
        P("pipe", None),
        P("pipe", None),
    )
    return jax.shard_map(
        local_program,
        mesh=mesh,
        in_specs=placed,
        out_specs=(P("pipe", "seq", None), P("seq", "pipe")),
        check_vma=False,
    )
```

```python
import functools

import jax
import jax.numpy as jnp
from jax import lax
from jax.experimental import pallas as pl
from jax.experimental.pallas import tpu as pltpu
from jax.sharding import PartitionSpec as P


F32, BF16 = jnp.float32, jnp.bfloat16


def dot(a, b):
    return lax.dot_general(a, b, (((1,), (0,)), ((), ())), preferred_element_type=F32)


def exchange(rows, devices):
    tile = rows.shape[0] // devices
    blocks = rows.reshape(devices, tile, rows.shape[1])
    blocks = lax.all_to_all(blocks, "seq", split_axis=0, concat_axis=0)
    return blocks.reshape(rows.shape)


def reorder_kernel(count, gain, rows_in, rows_out):
    order = rows_in.shape[0] // count
    chunk, tile = order // count, count * count
    n = lax.broadcasted_iota(jnp.int32, (order, order), 0)
    m = lax.broadcasted_iota(jnp.int32, (order, order), 1)
    place = (m == (n // count % count) * chunk + (n // tile) * count + n % count).astype(BF16)
    for group in range(count):
        starts = [il * order + group * chunk for il in range(count)]
        taken = jnp.concatenate([rows_in[s:s + chunk, :] for s in starts], axis=0)
        if gain is not None:
            taken = (taken.astype(F32) * gain[...].astype(F32)).astype(BF16)
        rows_out[group * order:(group + 1) * order, :] = dot(place, taken).astype(BF16)


def reorder(rows_in, count, gain=None):
    rows, channels = rows_in.shape
    width = min(1024, channels)
    specs = [pl.BlockSpec((rows, width), lambda n: (0, n))]
    operands = [rows_in]
    kernel = functools.partial(reorder_kernel, count, None)
    if gain is not None:
        specs.insert(0, pl.BlockSpec((1, width), lambda n: (0, n)))
        operands.insert(0, gain)
        kernel = functools.partial(reorder_kernel, count)
    return pl.pallas_call(
        kernel,
        out_shape=jax.ShapeDtypeStruct(rows_in.shape, BF16),
        grid=(channels // width,),
        in_specs=specs,
        out_specs=pl.BlockSpec((rows, width), lambda n: (0, n)),
        cost_estimate=pl.CostEstimate(
            flops=2 * rows * (rows // count) * channels, bytes_accessed=4 * rows * channels, transcendentals=0
        ),
    )(*operands)


def scale_kernel(flag, gain, here, moved, *rest):
    gradient = jnp.where(flag[0] == 1, here[...].astype(F32), moved[...].astype(F32))
    rest[-1][...] = (gradient * gain[...].astype(F32)).astype(BF16)


def scale_into(flag, gain, here, moved, total, at, buffer=None):
    rows, width = here.shape
    step, column = rows // 2, at // width
    block = pl.BlockSpec((step, width), lambda n: (n, 0))
    in_specs = [
        pl.BlockSpec(memory_space=pltpu.SMEM),
        pl.BlockSpec((1, width), lambda n: (0, 0)),
        block,
        block,
    ]
    operands = [flag, gain, here, moved]
    aliases = {}
    if buffer is not None:
        in_specs.append(pl.BlockSpec(memory_space=pl.ANY))
        operands.append(buffer)
        aliases = {4: 0}
    return pl.pallas_call(
        scale_kernel,
        out_shape=jax.ShapeDtypeStruct((rows, total), BF16),
        grid=(2,),
        in_specs=in_specs,
        out_specs=pl.BlockSpec((step, width), lambda n: (n, column)),
        input_output_aliases=aliases,
        cost_estimate=pl.CostEstimate(flops=rows * width, bytes_accessed=6 * rows * width, transcendentals=0),
    )(*operands)


def product_kernel(weights, columns, *rest):
    rest[-1][...] = dot(weights[...], columns[...]).astype(BF16)


def product_into(weights, columns, total, at, buffer=None):
    rows, depth = weights.shape
    width = min(512, columns.shape[1])
    steps, first = columns.shape[1] // width, at // width
    in_specs = [
        pl.BlockSpec((rows, depth), lambda n: (0, 0), pipeline_mode=pl.Buffered(1)),
        pl.BlockSpec((depth, width), lambda n: (0, n)),
    ]
    operands = [weights, columns]
    aliases = {}
    if buffer is not None:
        in_specs.append(pl.BlockSpec(memory_space=pl.ANY))
        operands.append(buffer)
        aliases = {2: 0}
    return pl.pallas_call(
        product_kernel,
        out_shape=jax.ShapeDtypeStruct((rows, total), BF16),
        grid=(steps,),
        in_specs=in_specs,
        out_specs=pl.BlockSpec((rows, width), lambda n: (0, first + n)),
        input_output_aliases=aliases,
        cost_estimate=pl.CostEstimate(
            flops=2 * rows * depth * columns.shape[1],
            bytes_accessed=2 * (rows * depth + 2 * rows * columns.shape[1]),
            transcendentals=0,
        ),
    )(*operands)


def local_program(arriving, loss_grad, first_blocks, second_blocks, inner_gain, outer_gain):
    sections = lax.axis_size("pipe")
    devices = lax.axis_size("seq")
    position = lax.axis_index("pipe")
    last = sections - 1
    first, second = first_blocks[0], second_blocks[0]
    count, order = first.shape[0], first.shape[1]
    rows, channels = arriving.shape[1:]
    piece = loss_grad.shape[1]
    tile = count * count

    out = lax.broadcasted_iota(jnp.int32, (rows, rows), 0)
    into = lax.broadcasted_iota(jnp.int32, (rows, rows), 1)
    natural = (out // count % count) * order + (out // tile) * count + out % count

    at = lax.broadcasted_iota(jnp.int32, (count, rows, order), 1)
    col = lax.broadcasted_iota(jnp.int32, (count, rows, order), 2)
    own = lax.broadcasted_iota(jnp.int32, (count, rows, order), 0)
    place = (at == col * count + own).astype(BF16)
    tall = jnp.einsum("jni,jki->nk", place, second, preferred_element_type=F32).astype(BF16)
    k = lax.broadcasted_iota(jnp.int32, (order, rows), 0)
    r = lax.broadcasted_iota(jnp.int32, (order, rows), 1)
    wide = dot(tall, (k == r // count).astype(BF16))
    second_spread = jnp.where(out % count == into % count, wide, 0.0).astype(BF16)

    pick = (k == (r // tile) * count + r % count).astype(BF16)
    wide = jnp.einsum("ikj,kr->ijr", first, pick, preferred_element_type=F32).reshape(rows, rows)
    first_spread = jnp.where(out // order == into // count % count, wide, 0.0).astype(BF16)

    inner, outer = inner_gain, outer_gain.astype(F32)
    restore = (natural.T == into.T).astype(BF16)
    first_sent = reorder(first_spread, count)

    def mix(columns):
        return dot(second_spread, columns).astype(BF16)

    def finish(gradient, weights, returned, cols):
        spread = dot(weights, returned)
        return (gradient.astype(F32) + outer[:, cols] * spread).astype(BF16)

    whole = slice(0, channels)
    halves = (slice(0, channels // 2), slice(channels // 2, channels))
    per_half = sections // 2

    first_sending = exchange(reorder(arriving[0], count, inner), devices)

    reordered = reorder(arriving[0], count)
    loss_sent = reorder(loss_grad, count)
    lost = [loss_sent if q == last else lax.ppermute(loss_sent, "pipe", [(q, last)]) for q in range(sections)]
    around = piece // sections
    cuts = ((0, piece - around, False), (piece - around, around, True), (piece, piece, False))
    here = [
        [lost[n * per_half + start // piece][:, start % piece:start % piece + width] for start, width, _ in cuts]
        for n in range(2)
    ]
    columns, here, first_sent, reordered = lax.optimization_barrier((first_sending, here, first_sent, reordered))

    back = [(i + 1, i) for i in range(sections - 1)]
    returned = [exchange(mix(columns[:, h]), devices) for h in halves]
    flag = (position == last).astype(jnp.int32).reshape(1)

    def shift(block, round_about):
        if not round_about:
            return lax.ppermute(block, "pipe", back)
        for hop in range(last):
            route = [((i + 1 + hop) % sections, (i + 2 + hop) % sections) for i in range(last)]
            block = lax.ppermute(block, "pipe", route)
        return block

    def step(n):
        passed, moved = [], []
        for c, (start, width, round_about) in enumerate(cuts):
            cols = slice(halves[n].start + start, halves[n].start + start + width)
            passed.append(finish(reordered[:, cols], first_sent, returned[n][:, start:start + width], cols))
            moved.append(shift(passed[c], round_about))
        return passed, moved

    def fill(n, moved):
        buffer = None
        for c in (1, 2, 0):
            start, width, _ = cuts[c]
            gain = inner[:, halves[n].start + start:halves[n].start + start + width]
            buffer = scale_into(flag, gain, here[n][c], moved[c], channels // 2, start, buffer)
        return buffer

    passed, moved, sent = [], [], []
    for n in range(2):
        done, shifted = step(n)
        sent.append(exchange(fill(n, shifted), devices))
        passed.append(done)
        moved += shifted

    leaving = jnp.concatenate(passed[0][:2], axis=1)
    for q in range(1, sections):
        parts = passed[q // per_half][:2] if q % per_half == 0 else passed[q // per_half][2:]
        parts = jnp.concatenate([lax.ppermute(p, "pipe", [(0, q)]) for p in parts], axis=1)
        leaving = jnp.where(position == q, parts, leaving)
    leaving = dot(restore, leaving).astype(BF16)

    mixed = product_into(second_spread, sent[0], channels, 0)
    mixed = product_into(second_spread, sent[1], channels, channels // 2, mixed)
    final = exchange(mixed, devices)
    source = jnp.concatenate([jnp.where(position == last, a, b) for a, b in zip(here[0] + here[1], moved)], axis=1)
    source = dot(restore, source).astype(BF16)
    final, source, leaving = lax.optimization_barrier((final, source, leaving))
    entering = finish(source, first_spread, final, whole)
    return entering[None], leaving


def solution(mesh):
    placed = (
        P("pipe", "seq", None),
        P("seq", "pipe"),
        P("pipe", "seq", None, None),
        P("pipe", "seq", None, None),
        P("pipe", None),
        P("pipe", None),
    )
    return jax.shard_map(
        local_program,
        mesh=mesh,
        in_specs=placed,
        out_specs=(P("pipe", "seq", None), P("seq", "pipe")),
        check_vma=False,
    )
```

```python
import functools

import jax
import jax.numpy as jnp
from jax import lax
from jax.experimental import pallas as pl
from jax.experimental.pallas import tpu as pltpu
from jax.sharding import PartitionSpec as P


F32, BF16 = jnp.float32, jnp.bfloat16


def dot(a, b):
    return lax.dot_general(a, b, (((1,), (0,)), ((), ())), preferred_element_type=F32)


def exchange(rows, devices):
    tile = rows.shape[0] // devices
    blocks = rows.reshape(devices, tile, rows.shape[1])
    blocks = lax.all_to_all(blocks, "seq", split_axis=0, concat_axis=0)
    return blocks.reshape(rows.shape)


def reorder_kernel(count, gain, rows_in, rows_out):
    order = rows_in.shape[0] // count
    chunk, tile = order // count, count * count
    n = lax.broadcasted_iota(jnp.int32, (order, order), 0)
    m = lax.broadcasted_iota(jnp.int32, (order, order), 1)
    place = (m == (n // count % count) * chunk + (n // tile) * count + n % count).astype(BF16)
    for group in range(count):
        starts = [il * order + group * chunk for il in range(count)]
        taken = jnp.concatenate([rows_in[s:s + chunk, :] for s in starts], axis=0)
        if gain is not None:
            taken = (taken.astype(F32) * gain[...].astype(F32)).astype(BF16)
        rows_out[group * order:(group + 1) * order, :] = dot(place, taken).astype(BF16)


def reorder(rows_in, count, gain=None):
    rows, channels = rows_in.shape
    width = min(1024, channels)
    specs = [pl.BlockSpec((rows, width), lambda n: (0, n))]
    operands = [rows_in]
    kernel = functools.partial(reorder_kernel, count, None)
    if gain is not None:
        specs.insert(0, pl.BlockSpec((1, width), lambda n: (0, n)))
        operands.insert(0, gain)
        kernel = functools.partial(reorder_kernel, count)
    return pl.pallas_call(
        kernel,
        out_shape=jax.ShapeDtypeStruct(rows_in.shape, BF16),
        grid=(channels // width,),
        in_specs=specs,
        out_specs=pl.BlockSpec((rows, width), lambda n: (0, n)),
        cost_estimate=pl.CostEstimate(
            flops=2 * rows * (rows // count) * channels, bytes_accessed=4 * rows * channels, transcendentals=0
        ),
    )(*operands)


def restore_kernel(count, rows_in, rows_out):
    order = rows_in.shape[0] // count
    chunk, tile = order // count, count * count
    m = lax.broadcasted_iota(jnp.int32, (order, order), 0)
    n = lax.broadcasted_iota(jnp.int32, (order, order), 1)
    place = (m == (n // count % count) * chunk + (n // tile) * count + n % count).astype(BF16)
    for group in range(count):
        placed = dot(place, rows_in[group * order:(group + 1) * order, :]).astype(BF16)
        for il in range(count):
            start = il * order + group * chunk
            rows_out[start:start + chunk, :] = placed[il * chunk:(il + 1) * chunk, :]


def restore(rows_in, count):
    rows, channels = rows_in.shape
    width = min(1024, channels)
    block = pl.BlockSpec((rows, width), lambda n: (0, n))
    return pl.pallas_call(
        functools.partial(restore_kernel, count),
        out_shape=jax.ShapeDtypeStruct(rows_in.shape, BF16),
        grid=(channels // width,),
        in_specs=[block],
        out_specs=block,
        cost_estimate=pl.CostEstimate(
            flops=2 * rows * (rows // count) * channels, bytes_accessed=4 * rows * channels, transcendentals=0
        ),
    )(rows_in)


def scale_kernel(flag, gain, here, moved, *rest):
    gradient = jnp.where(flag[0] == 1, here[...].astype(F32), moved[...].astype(F32))
    rest[-1][...] = (gradient * gain[...].astype(F32)).astype(BF16)


def scale_into(flag, gain, here, moved, total, at, buffer=None):
    rows, width = here.shape
    step, column = rows // 2, at // width
    block = pl.BlockSpec((step, width), lambda n: (n, 0))
    in_specs = [
        pl.BlockSpec(memory_space=pltpu.SMEM),
        pl.BlockSpec((1, width), lambda n: (0, 0)),
        block,
        block,
    ]
    operands = [flag, gain, here, moved]
    aliases = {}
    if buffer is not None:
        in_specs.append(pl.BlockSpec(memory_space=pl.ANY))
        operands.append(buffer)
        aliases = {4: 0}
    return pl.pallas_call(
        scale_kernel,
        out_shape=jax.ShapeDtypeStruct((rows, total), BF16),
        grid=(2,),
        in_specs=in_specs,
        out_specs=pl.BlockSpec((step, width), lambda n: (n, column)),
        input_output_aliases=aliases,
        cost_estimate=pl.CostEstimate(flops=rows * width, bytes_accessed=6 * rows * width, transcendentals=0),
    )(*operands)


def product_kernel(weights, columns, *rest):
    rest[-1][...] = dot(weights[...], columns[...]).astype(BF16)


def product_into(weights, columns, taken, total, at, buffer=None):
    rows, depth = weights.shape
    count = taken.stop - taken.start
    width = min(512, count)
    steps, source, first = count // width, taken.start // width, at // width
    in_specs = [
        pl.BlockSpec((rows, depth), lambda n: (0, 0), pipeline_mode=pl.Buffered(1)),
        pl.BlockSpec((depth, width), lambda n: (0, source + n)),
    ]
    operands = [weights, columns]
    aliases = {}
    if buffer is not None:
        in_specs.append(pl.BlockSpec(memory_space=pl.ANY))
        operands.append(buffer)
        aliases = {2: 0}
    return pl.pallas_call(
        product_kernel,
        out_shape=jax.ShapeDtypeStruct((rows, total), BF16),
        grid=(steps,),
        in_specs=in_specs,
        out_specs=pl.BlockSpec((rows, width), lambda n: (0, first + n)),
        input_output_aliases=aliases,
        cost_estimate=pl.CostEstimate(
            flops=2 * rows * depth * count,
            bytes_accessed=2 * (rows * depth + 2 * rows * count),
            transcendentals=0,
        ),
    )(*operands)


def local_program(arriving, loss_grad, first_blocks, second_blocks, inner_gain, outer_gain):
    sections = lax.axis_size("pipe")
    devices = lax.axis_size("seq")
    position = lax.axis_index("pipe")
    last = sections - 1
    first, second = first_blocks[0], second_blocks[0]
    count, order = first.shape[0], first.shape[1]
    rows, channels = arriving.shape[1:]
    piece = loss_grad.shape[1]
    tile = count * count

    out = lax.broadcasted_iota(jnp.int32, (rows, rows), 0)
    into = lax.broadcasted_iota(jnp.int32, (rows, rows), 1)

    at = lax.broadcasted_iota(jnp.int32, (count, rows, order), 1)
    col = lax.broadcasted_iota(jnp.int32, (count, rows, order), 2)
    own = lax.broadcasted_iota(jnp.int32, (count, rows, order), 0)
    place = (at == col * count + own).astype(BF16)
    tall = jnp.einsum("jni,jki->nk", place, second, preferred_element_type=F32).astype(BF16)
    k = lax.broadcasted_iota(jnp.int32, (order, rows), 0)
    r = lax.broadcasted_iota(jnp.int32, (order, rows), 1)
    wide = dot(tall, (k == r // count).astype(BF16))
    second_spread = jnp.where(out % count == into % count, wide, 0.0).astype(BF16)

    pick = (k == (r // tile) * count + r % count).astype(BF16)
    wide = jnp.einsum("ikj,kr->ijr", first, pick, preferred_element_type=F32).reshape(rows, rows)
    first_spread = jnp.where(out // order == into // count % count, wide, 0.0).astype(BF16)

    inner, outer = inner_gain, outer_gain.astype(F32)
    first_sent = reorder(first_spread, count)

    def finish(gradient, weights, returned, cols):
        spread = dot(weights, returned)
        return (gradient.astype(F32) + outer[:, cols] * spread).astype(BF16)

    whole = slice(0, channels)
    halves = (slice(0, channels // 2), slice(channels // 2, channels))
    per_half = sections // 2

    first_sending = exchange(reorder(arriving[0], count, inner), devices)

    reordered = reorder(arriving[0], count)
    loss_sent = reorder(loss_grad, count)
    lost = [loss_sent if q == last else lax.ppermute(loss_sent, "pipe", [(q, last)]) for q in range(sections)]
    around = piece // 4
    cuts = (
        (0, 2 * around, False),
        (2 * around, around, True),
        (3 * around, around, True),
        (piece, piece, False),
    )
    here = [
        [lost[n * per_half + start // piece][:, start % piece:start % piece + width] for start, width, _ in cuts]
        for n in range(2)
    ]
    columns, here, first_sent, reordered = lax.optimization_barrier((first_sending, here, first_sent, reordered))

    back = [(i + 1, i) for i in range(sections - 1)]
    returned = [exchange(product_into(second_spread, columns, h, channels // 2, 0), devices) for h in halves]
    flag = (position == last).astype(jnp.int32).reshape(1)

    def shift(block, round_about):
        if not round_about:
            return lax.ppermute(block, "pipe", back)
        for hop in range(last):
            route = [((i + 1 + hop) % sections, (i + 2 + hop) % sections) for i in range(last)]
            block = lax.ppermute(block, "pipe", route)
        return block

    def step(n):
        passed, moved = [], []
        for c, (start, width, round_about) in enumerate(cuts):
            cols = slice(halves[n].start + start, halves[n].start + start + width)
            passed.append(finish(reordered[:, cols], first_sent, returned[n][:, start:start + width], cols))
            moved.append(shift(passed[c], round_about))
        return passed, moved

    def fill(n, moved):
        buffer = None
        for c, (start, width, _) in enumerate(cuts):
            gain = inner[:, halves[n].start + start:halves[n].start + start + width]
            buffer = scale_into(flag, gain, here[n][c], moved[c], channels // 2, start, buffer)
        return buffer

    passed, moved, sent = [], [], []
    for n in range(2):
        done, shifted = step(n)
        sent.append(exchange(fill(n, shifted), devices))
        passed.append(done)
        moved += shifted

    leaving = jnp.concatenate(passed[0][:-1], axis=1)
    for q in range(1, sections):
        parts = passed[q // per_half][:-1] if q % per_half == 0 else passed[q // per_half][-1:]
        parts = lax.ppermute(jnp.concatenate(parts, axis=1), "pipe", [(0, q)])
        leaving = jnp.where(position == q, parts, leaving)
    leaving = restore(leaving, count)

    mixed = product_into(second_spread, sent[0], slice(0, channels // 2), channels, 0)
    mixed = product_into(second_spread, sent[1], slice(0, channels // 2), channels, channels // 2, mixed)
    final = exchange(mixed, devices)
    source = jnp.concatenate([jnp.where(position == last, a, b) for a, b in zip(here[0] + here[1], moved)], axis=1)
    source = restore(source, count)
    final, source, leaving = lax.optimization_barrier((final, source, leaving))
    entering = finish(source, first_spread, final, whole)
    return entering[None], leaving


def solution(mesh):
    placed = (
        P("pipe", "seq", None),
        P("seq", "pipe"),
        P("pipe", "seq", None, None),
        P("pipe", "seq", None, None),
        P("pipe", None),
        P("pipe", None),
    )
    return jax.shard_map(
        local_program,
        mesh=mesh,
        in_specs=placed,
        out_specs=(P("pipe", "seq", None), P("seq", "pipe")),
        check_vma=False,
    )
```

```python
import functools

import jax
import jax.numpy as jnp
from jax import lax
from jax.experimental import pallas as pl
from jax.experimental.pallas import tpu as pltpu
from jax.sharding import PartitionSpec as P


F32, BF16 = jnp.float32, jnp.bfloat16


def dot(a, b):
    return lax.dot_general(a, b, (((1,), (0,)), ((), ())), preferred_element_type=F32)


def exchange(rows, devices):
    tile = rows.shape[0] // devices
    blocks = rows.reshape(devices, tile, rows.shape[1])
    blocks = lax.all_to_all(blocks, "seq", split_axis=0, concat_axis=0)
    return blocks.reshape(rows.shape)


def sent_to_natural(count, order):
    chunk, tile = order // count, count * count
    m = lax.broadcasted_iota(jnp.int32, (order, order), 0)
    n = lax.broadcasted_iota(jnp.int32, (order, order), 1)
    return (m == (n // count % count) * chunk + (n // tile) * count + n % count).astype(BF16)


def reorder_kernel(count, gain, rows_in, rows_out):
    order = rows_in.shape[0] // count
    chunk, tile = order // count, count * count
    n = lax.broadcasted_iota(jnp.int32, (order, order), 0)
    m = lax.broadcasted_iota(jnp.int32, (order, order), 1)
    place = (m == (n // count % count) * chunk + (n // tile) * count + n % count).astype(BF16)
    for group in range(count):
        starts = [il * order + group * chunk for il in range(count)]
        taken = jnp.concatenate([rows_in[s:s + chunk, :] for s in starts], axis=0)
        if gain is not None:
            taken = (taken.astype(F32) * gain[...].astype(F32)).astype(BF16)
        rows_out[group * order:(group + 1) * order, :] = dot(place, taken).astype(BF16)


def reorder(rows_in, count, gain=None):
    rows, channels = rows_in.shape
    width = min(1024, channels)
    specs = [pl.BlockSpec((rows, width), lambda n: (0, n))]
    operands = [rows_in]
    kernel = functools.partial(reorder_kernel, count, None)
    if gain is not None:
        specs.insert(0, pl.BlockSpec((1, width), lambda n: (0, n)))
        operands.insert(0, gain)
        kernel = functools.partial(reorder_kernel, count)
    return pl.pallas_call(
        kernel,
        out_shape=jax.ShapeDtypeStruct(rows_in.shape, BF16),
        grid=(channels // width,),
        in_specs=specs,
        out_specs=pl.BlockSpec((rows, width), lambda n: (0, n)),
        cost_estimate=pl.CostEstimate(
            flops=2 * rows * (rows // count) * channels, bytes_accessed=4 * rows * channels, transcendentals=0
        ),
    )(*operands)


def restore_kernel(count, rows_in, rows_out):
    placed = dot(sent_to_natural(count, rows_in.shape[0]), rows_in[...]).astype(BF16)
    rows_out[...] = placed.reshape(rows_out.shape)


def restore(rows_in, count):
    rows, channels = rows_in.shape
    order = rows // count
    return pl.pallas_call(
        functools.partial(restore_kernel, count),
        out_shape=jax.ShapeDtypeStruct((count, order, channels), BF16),
        grid=(count,),
        in_specs=[pl.BlockSpec((order, channels), lambda n: (n, 0))],
        out_specs=pl.BlockSpec((count, order // count, channels), lambda n: (0, n, 0)),
        cost_estimate=pl.CostEstimate(
            flops=2 * rows * order * channels, bytes_accessed=4 * rows * channels, transcendentals=0
        ),
    )(rows_in).reshape(rows_in.shape)


def final_kernel(count, factors, columns, source, gain, result):
    order = factors.shape[1]
    chunk = order // count
    place = sent_to_natural(count, order)
    groups = [dot(place, columns[g * order:(g + 1) * order, :]).astype(BF16) for g in range(count)]
    for il in range(count):
        mine = jnp.concatenate([g[il * chunk:(il + 1) * chunk, :] for g in groups], axis=0)
        spread = dot(factors[il], mine)
        part = slice(il * order, (il + 1) * order)
        result[part, :] = (source[part, :].astype(F32) + gain[...] * spread).astype(BF16)


def final_product(factors, columns, source, gain, width=512):
    count, order = factors.shape[:2]
    rows, channels = columns.shape
    block = pl.BlockSpec((rows, width), lambda n: (0, n))
    return pl.pallas_call(
        functools.partial(final_kernel, count),
        out_shape=jax.ShapeDtypeStruct((rows, channels), BF16),
        grid=(channels // width,),
        in_specs=[
            pl.BlockSpec(factors.shape, lambda n: (0, 0, 0), pipeline_mode=pl.Buffered(1)),
            block,
            block,
            pl.BlockSpec((1, width), lambda n: (0, n)),
        ],
        out_specs=block,
        cost_estimate=pl.CostEstimate(
            flops=4 * rows * order * channels, bytes_accessed=6 * rows * channels, transcendentals=0
        ),
    )(factors, columns, source, gain)


def scale_kernel(flag, gain, here, moved, *rest):
    gradient = jnp.where(flag[0] == 1, here[...].astype(F32), moved[...].astype(F32))
    rest[-1][...] = (gradient * gain[...].astype(F32)).astype(BF16)


def scale_into(flag, gain, here, moved, total, at, buffer=None):
    rows, width = here.shape
    unit = min(256, width)
    step, column = rows // 2, at // unit
    block = pl.BlockSpec((step, unit), lambda n, m: (n, m))
    in_specs = [
        pl.BlockSpec(memory_space=pltpu.SMEM),
        pl.BlockSpec((1, unit), lambda n, m: (0, m)),
        block,
        block,
    ]
    operands = [flag, gain, here, moved]
    aliases = {}
    if buffer is not None:
        in_specs.append(pl.BlockSpec(memory_space=pl.ANY))
        operands.append(buffer)
        aliases = {4: 0}
    return pl.pallas_call(
        scale_kernel,
        out_shape=jax.ShapeDtypeStruct((rows, total), BF16),
        grid=(2, width // unit),
        in_specs=in_specs,
        out_specs=pl.BlockSpec((step, unit), lambda n, m: (n, column + m)),
        input_output_aliases=aliases,
        cost_estimate=pl.CostEstimate(flops=rows * width, bytes_accessed=6 * rows * width, transcendentals=0),
    )(*operands)


def product_kernel(weights, columns, *rest):
    rest[-1][...] = dot(weights[...], columns[...]).astype(BF16)


def product_into(weights, columns, total, at, buffer=None):
    rows, depth = weights.shape
    width = min(512, columns.shape[1])
    steps, first = columns.shape[1] // width, at // width
    in_specs = [
        pl.BlockSpec((rows, depth), lambda n: (0, 0), pipeline_mode=pl.Buffered(1)),
        pl.BlockSpec((depth, width), lambda n: (0, n)),
    ]
    operands = [weights, columns]
    aliases = {}
    if buffer is not None:
        in_specs.append(pl.BlockSpec(memory_space=pl.ANY))
        operands.append(buffer)
        aliases = {2: 0}
    return pl.pallas_call(
        product_kernel,
        out_shape=jax.ShapeDtypeStruct((rows, total), BF16),
        grid=(steps,),
        in_specs=in_specs,
        out_specs=pl.BlockSpec((rows, width), lambda n: (0, first + n)),
        input_output_aliases=aliases,
        cost_estimate=pl.CostEstimate(
            flops=2 * rows * depth * columns.shape[1],
            bytes_accessed=2 * (rows * depth + 2 * rows * columns.shape[1]),
            transcendentals=0,
        ),
    )(*operands)


def local_program(arriving, loss_grad, first_blocks, second_blocks, inner_gain, outer_gain):
    sections = lax.axis_size("pipe")
    devices = lax.axis_size("seq")
    position = lax.axis_index("pipe")
    last = sections - 1
    first, second = first_blocks[0], second_blocks[0]
    count, order = first.shape[0], first.shape[1]
    rows, channels = arriving.shape[1:]
    piece = loss_grad.shape[1]
    tile = count * count

    out = lax.broadcasted_iota(jnp.int32, (rows, rows), 0)
    into = lax.broadcasted_iota(jnp.int32, (rows, rows), 1)

    at = lax.broadcasted_iota(jnp.int32, (count, rows, order), 1)
    col = lax.broadcasted_iota(jnp.int32, (count, rows, order), 2)
    own = lax.broadcasted_iota(jnp.int32, (count, rows, order), 0)
    place = (at == col * count + own).astype(BF16)
    tall = jnp.einsum("jni,jki->nk", place, second, preferred_element_type=F32).astype(BF16)
    k = lax.broadcasted_iota(jnp.int32, (order, rows), 0)
    r = lax.broadcasted_iota(jnp.int32, (order, rows), 1)
    wide = dot(tall, (k == r // count).astype(BF16))
    second_spread = jnp.where(out % count == into % count, wide, 0.0).astype(BF16)

    pick = (k == (r // tile) * count + r % count).astype(BF16)
    wide = jnp.einsum("ikj,kr->ijr", first, pick, preferred_element_type=F32).reshape(rows, rows)
    first_spread = jnp.where(out // order == into // count % count, wide, 0.0).astype(BF16)

    inner, outer = inner_gain, outer_gain.astype(F32)
    first_sent = reorder(first_spread, count)

    def mix(columns):
        return dot(second_spread, columns).astype(BF16)

    def finish(gradient, weights, returned, cols):
        spread = dot(weights, returned)
        return (gradient.astype(F32) + outer[:, cols] * spread).astype(BF16)

    halves = (slice(0, channels // 2), slice(channels // 2, channels))
    per_half = sections // 2

    first_sending = exchange(reorder(arriving[0], count, inner), devices)

    reordered = reorder(arriving[0], count)
    loss_sent = reorder(loss_grad, count)
    lost = [loss_sent if q == last else lax.ppermute(loss_sent, "pipe", [(q, last)]) for q in range(sections)]
    cuts = ((0, piece // 2), (piece // 2, piece), (piece // 2 + piece, piece // 2))
    here = []
    for n in range(2):
        both = jnp.concatenate(lost[n * per_half:(n + 1) * per_half], axis=1)
        here.append([both[:, start:start + width] for start, width in cuts])
    turned = jnp.swapaxes(first, 1, 2)
    columns, here, first_sent, reordered, turned = lax.optimization_barrier(
        (first_sending, here, first_sent, reordered, turned)
    )

    back = [(i + 1, i) for i in range(sections - 1)]
    returned = [exchange(mix(columns[:, h]), devices) for h in halves]
    flag = (position == last).astype(jnp.int32).reshape(1)

    def step(n):
        passed, moved = [], []
        for c, (start, width) in enumerate(cuts):
            cols = slice(halves[n].start + start, halves[n].start + start + width)
            passed.append(finish(reordered[:, cols], first_sent, returned[n][:, start:start + width], cols))
            moved.append(lax.ppermute(passed[c], "pipe", back))
        return passed, moved

    def fill(n, moved):
        buffer = None
        for c, (start, width) in enumerate(cuts):
            gain = inner[:, halves[n].start + start:halves[n].start + start + width]
            buffer = scale_into(flag, gain, here[n][c], moved[c], channels // 2, start, buffer)
        return buffer

    passed, moved, sent = [], [], []
    for n in range(2):
        done, shifted = step(n)
        sent.append(exchange(fill(n, shifted), devices))
        passed.append(jnp.concatenate(done, axis=1))
        moved += shifted

    leaving = passed[0][:, :piece]
    for q in range(1, sections):
        start = q % per_half * piece
        part = lax.ppermute(passed[q // per_half][:, start:start + piece], "pipe", [(0, q)])
        leaving = jnp.where(position == q, part, leaving)
    leaving = restore(leaving, count)

    mixed = product_into(second_spread, sent[0], channels, 0)
    mixed = product_into(second_spread, sent[1], channels, channels // 2, mixed)
    final = exchange(mixed, devices)
    source = jnp.concatenate([jnp.where(position == last, a, b) for a, b in zip(here[0] + here[1], moved)], axis=1)
    source = restore(source, count)
    final, source, leaving = lax.optimization_barrier((final, source, leaving))
    entering = final_product(turned, final, source, outer)
    return entering[None], leaving


def solution(mesh):
    placed = (
        P("pipe", "seq", None),
        P("seq", "pipe"),
        P("pipe", "seq", None, None),
        P("pipe", "seq", None, None),
        P("pipe", None),
        P("pipe", None),
    )
    return jax.shard_map(
        local_program,
        mesh=mesh,
        in_specs=placed,
        out_specs=(P("pipe", "seq", None), P("seq", "pipe")),
        check_vma=False,
    )
```

```python
import functools

import jax
import jax.numpy as jnp
from jax import lax
from jax.experimental import pallas as pl
from jax.experimental.pallas import tpu as pltpu
from jax.sharding import PartitionSpec as P


F32, BF16 = jnp.float32, jnp.bfloat16


def dot(a, b):
    return lax.dot_general(a, b, (((1,), (0,)), ((), ())), preferred_element_type=F32)


def exchange(rows, devices):
    tile = rows.shape[0] // devices
    blocks = rows.reshape(devices, tile, rows.shape[1])
    blocks = lax.all_to_all(blocks, "seq", split_axis=0, concat_axis=0)
    return blocks.reshape(rows.shape)


def sent_to_natural(count, order):
    chunk, tile = order // count, count * count
    m = lax.broadcasted_iota(jnp.int32, (order, order), 0)
    n = lax.broadcasted_iota(jnp.int32, (order, order), 1)
    return (m == (n // count % count) * chunk + (n // tile) * count + n % count).astype(BF16)


def reorder_kernel(count, gain, rows_in, rows_out):
    order = rows_in.shape[0] // count
    chunk, tile = order // count, count * count
    n = lax.broadcasted_iota(jnp.int32, (order, order), 0)
    m = lax.broadcasted_iota(jnp.int32, (order, order), 1)
    place = (m == (n // count % count) * chunk + (n // tile) * count + n % count).astype(BF16)
    for group in range(count):
        starts = [il * order + group * chunk for il in range(count)]
        taken = jnp.concatenate([rows_in[s:s + chunk, :] for s in starts], axis=0)
        if gain is not None:
            taken = (taken.astype(F32) * gain[...].astype(F32)).astype(BF16)
        rows_out[group * order:(group + 1) * order, :] = dot(place, taken).astype(BF16)


def reorder(rows_in, count, gain=None):
    rows, channels = rows_in.shape
    width = min(1024, channels)
    specs = [pl.BlockSpec((rows, width), lambda n: (0, n))]
    operands = [rows_in]
    kernel = functools.partial(reorder_kernel, count, None)
    if gain is not None:
        specs.insert(0, pl.BlockSpec((1, width), lambda n: (0, n)))
        operands.insert(0, gain)
        kernel = functools.partial(reorder_kernel, count)
    return pl.pallas_call(
        kernel,
        out_shape=jax.ShapeDtypeStruct(rows_in.shape, BF16),
        grid=(channels // width,),
        in_specs=specs,
        out_specs=pl.BlockSpec((rows, width), lambda n: (0, n)),
        cost_estimate=pl.CostEstimate(
            flops=2 * rows * (rows // count) * channels, bytes_accessed=4 * rows * channels, transcendentals=0
        ),
    )(*operands)


def restore_kernel(count, rows_in, rows_out):
    placed = dot(sent_to_natural(count, rows_in.shape[0]), rows_in[...]).astype(BF16)
    rows_out[...] = placed.reshape(rows_out.shape)


def restore(rows_in, count):
    rows, channels = rows_in.shape
    order = rows // count
    return pl.pallas_call(
        functools.partial(restore_kernel, count),
        out_shape=jax.ShapeDtypeStruct((count, order, channels), BF16),
        grid=(count,),
        in_specs=[pl.BlockSpec((order, channels), lambda n: (n, 0))],
        out_specs=pl.BlockSpec((count, order // count, channels), lambda n: (0, n, 0)),
        cost_estimate=pl.CostEstimate(
            flops=2 * rows * order * channels, bytes_accessed=4 * rows * channels, transcendentals=0
        ),
    )(rows_in).reshape(rows_in.shape)


def final_kernel(count, factors, columns, source, gain, result):
    order = factors.shape[1]
    chunk = order // count
    place = sent_to_natural(count, order)
    groups = [dot(place, columns[g * order:(g + 1) * order, :]).astype(BF16) for g in range(count)]
    for il in range(count):
        mine = jnp.concatenate([g[il * chunk:(il + 1) * chunk, :] for g in groups], axis=0)
        spread = dot(factors[il], mine)
        part = slice(il * order, (il + 1) * order)
        result[part, :] = (source[part, :].astype(F32) + gain[...] * spread).astype(BF16)


def final_product(factors, columns, source, gain, width=512):
    count, order = factors.shape[:2]
    rows, channels = columns.shape
    block = pl.BlockSpec((rows, width), lambda n: (0, n))
    return pl.pallas_call(
        functools.partial(final_kernel, count),
        out_shape=jax.ShapeDtypeStruct((rows, channels), BF16),
        grid=(channels // width,),
        in_specs=[
            pl.BlockSpec(factors.shape, lambda n: (0, 0, 0), pipeline_mode=pl.Buffered(1)),
            block,
            block,
            pl.BlockSpec((1, width), lambda n: (0, n)),
        ],
        out_specs=block,
        cost_estimate=pl.CostEstimate(
            flops=4 * rows * order * channels, bytes_accessed=6 * rows * channels, transcendentals=0
        ),
    )(factors, columns, source, gain)


def scale_kernel(flag, gain, here, moved, *rest):
    gradient = jnp.where(flag[0] == 1, here[...].astype(F32), moved[...].astype(F32))
    rest[-1][...] = (gradient * gain[...].astype(F32)).astype(BF16)


def scale_into(flag, gain, here, moved, total, at, buffer=None):
    rows, width = here.shape
    unit = min(256, width)
    step, column = rows // 2, at // unit
    block = pl.BlockSpec((step, unit), lambda n, m: (n, m))
    in_specs = [
        pl.BlockSpec(memory_space=pltpu.SMEM),
        pl.BlockSpec((1, unit), lambda n, m: (0, m)),
        block,
        block,
    ]
    operands = [flag, gain, here, moved]
    aliases = {}
    if buffer is not None:
        in_specs.append(pl.BlockSpec(memory_space=pl.ANY))
        operands.append(buffer)
        aliases = {4: 0}
    return pl.pallas_call(
        scale_kernel,
        out_shape=pltpu.HBM((rows, total), BF16),
        grid=(2, width // unit),
        in_specs=in_specs,
        out_specs=pl.BlockSpec((step, unit), lambda n, m: (n, column + m)),
        input_output_aliases=aliases,
        cost_estimate=pl.CostEstimate(flops=rows * width, bytes_accessed=6 * rows * width, transcendentals=0),
        compiler_params=pltpu.CompilerParams(vmem_limit_bytes=24 * 2**20),
    )(*operands)


def product_kernel(weights, columns, *rest):
    rest[-1][...] = dot(weights[...], columns[...]).astype(BF16)


def product_into(weights, columns, total, at, buffer=None):
    rows, depth = weights.shape
    width = min(512, columns.shape[1])
    steps, first = columns.shape[1] // width, at // width
    in_specs = [
        pl.BlockSpec((rows, depth), lambda n: (0, 0), pipeline_mode=pl.Buffered(1)),
        pl.BlockSpec((depth, width), lambda n: (0, n)),
    ]
    operands = [pltpu.with_memory_space_constraint(weights, pltpu.HBM), columns]
    aliases = {}
    if buffer is not None:
        in_specs.append(pl.BlockSpec(memory_space=pl.ANY))
        operands.append(buffer)
        aliases = {2: 0}
    return pl.pallas_call(
        product_kernel,
        out_shape=pltpu.HBM((rows, total), BF16),
        grid=(steps,),
        in_specs=in_specs,
        out_specs=pl.BlockSpec((rows, width), lambda n: (0, first + n)),
        input_output_aliases=aliases,
        cost_estimate=pl.CostEstimate(
            flops=2 * rows * depth * columns.shape[1],
            bytes_accessed=2 * (rows * depth + 2 * rows * columns.shape[1]),
            transcendentals=0,
        ),
        compiler_params=pltpu.CompilerParams(vmem_limit_bytes=24 * 2**20),
    )(*operands)


def local_program(arriving, loss_grad, first_blocks, second_blocks, inner_gain, outer_gain):
    sections = lax.axis_size("pipe")
    devices = lax.axis_size("seq")
    position = lax.axis_index("pipe")
    last = sections - 1
    first, second = first_blocks[0], second_blocks[0]
    count, order = first.shape[0], first.shape[1]
    rows, channels = arriving.shape[1:]
    piece = loss_grad.shape[1]
    tile = count * count

    out = lax.broadcasted_iota(jnp.int32, (rows, rows), 0)
    into = lax.broadcasted_iota(jnp.int32, (rows, rows), 1)

    at = lax.broadcasted_iota(jnp.int32, (count, rows, order), 1)
    col = lax.broadcasted_iota(jnp.int32, (count, rows, order), 2)
    own = lax.broadcasted_iota(jnp.int32, (count, rows, order), 0)
    place = (at == col * count + own).astype(BF16)
    tall = jnp.einsum("jni,jki->nk", place, second, preferred_element_type=F32).astype(BF16)
    k = lax.broadcasted_iota(jnp.int32, (order, rows), 0)
    r = lax.broadcasted_iota(jnp.int32, (order, rows), 1)
    wide = dot(tall, (k == r // count).astype(BF16))
    second_spread = jnp.where(out % count == into % count, wide, 0.0).astype(BF16)

    pick = (k == (r // tile) * count + r % count).astype(BF16)
    wide = jnp.einsum("ikj,kr->ijr", first, pick, preferred_element_type=F32).reshape(rows, rows)
    first_spread = jnp.where(out // order == into // count % count, wide, 0.0).astype(BF16)

    inner, outer = inner_gain, outer_gain.astype(F32)
    first_sent = reorder(first_spread, count)

    def mix(columns):
        return dot(second_spread, columns).astype(BF16)

    def finish(gradient, weights, returned, cols):
        spread = dot(weights, returned)
        return (gradient.astype(F32) + outer[:, cols] * spread).astype(BF16)

    halves = (slice(0, channels // 2), slice(channels // 2, channels))
    per_half = sections // 2

    first_sending = exchange(reorder(arriving[0], count, inner), devices)

    reordered = reorder(arriving[0], count)
    loss_sent = reorder(loss_grad, count)
    lost = [loss_sent if q == last else lax.ppermute(loss_sent, "pipe", [(q, last)]) for q in range(sections)]
    cuts = ((0, piece // 2), (piece // 2, piece), (piece // 2 + piece, piece // 2))
    here = []
    for n in range(2):
        both = jnp.concatenate(lost[n * per_half:(n + 1) * per_half], axis=1)
        here.append([both[:, start:start + width] for start, width in cuts])
    turned = jnp.swapaxes(first, 1, 2)
    columns, here, first_sent, reordered, turned = lax.optimization_barrier(
        (first_sending, here, first_sent, reordered, turned)
    )

    back = [(i + 1, i) for i in range(sections - 1)]
    returned = [exchange(mix(columns[:, h]), devices) for h in halves]
    flag = (position == last).astype(jnp.int32).reshape(1)

    def step(n):
        passed, moved = [], []
        for c, (start, width) in enumerate(cuts):
            cols = slice(halves[n].start + start, halves[n].start + start + width)
            passed.append(finish(reordered[:, cols], first_sent, returned[n][:, start:start + width], cols))
            moved.append(lax.ppermute(passed[c], "pipe", back))
        return passed, moved

    def fill(n, moved):
        buffer = None
        for c, (start, width) in enumerate(cuts):
            gain = inner[:, halves[n].start + start:halves[n].start + start + width]
            buffer = scale_into(flag, gain, here[n][c], moved[c], channels // 2, start, buffer)
        return buffer

    passed, moved, sent = [], [], []
    for n in range(2):
        done, shifted = step(n)
        sent.append(exchange(fill(n, shifted), devices))
        passed.append(jnp.concatenate(done, axis=1))
        moved += shifted

    leaving = passed[0][:, :piece]
    for q in range(1, sections):
        start = q % per_half * piece
        part = lax.ppermute(passed[q // per_half][:, start:start + piece], "pipe", [(0, q)])
        leaving = jnp.where(position == q, part, leaving)
    leaving = restore(leaving, count)

    mixed = product_into(second_spread, sent[0], channels, 0)
    mixed = product_into(second_spread, sent[1], channels, channels // 2, mixed)
    final = exchange(mixed, devices)
    source = jnp.concatenate([jnp.where(position == last, a, b) for a, b in zip(here[0] + here[1], moved)], axis=1)
    source = restore(source, count)
    final, source, leaving = lax.optimization_barrier((final, source, leaving))
    entering = final_product(turned, final, source, outer)
    return entering[None], leaving


def solution(mesh):
    placed = (
        P("pipe", "seq", None),
        P("seq", "pipe"),
        P("pipe", "seq", None, None),
        P("pipe", "seq", None, None),
        P("pipe", None),
        P("pipe", None),
    )
    return jax.shard_map(
        local_program,
        mesh=mesh,
        in_specs=placed,
        out_specs=(P("pipe", "seq", None), P("seq", "pipe")),
        check_vma=False,
    )
```
